32 devices in a mesh: grp: 16 (over z, x, core), gy: 2 (over y).
Axes of the slice: x: 2, y: 2, z: 4, core: 2. Of those that a mesh axis runs over, the one named last changes fastest.
Arguments:
- potential_warmth: float32 [24, 256, 1024], P(None, 'grp', 'gy'), may hold values from -2 to 4
- saltiness_anomaly: float32 [24, 256, 1024], P(None, 'grp', 'gy'), may hold values from -6 to 6
- seawater_velocity: float32 [2, 256, 1024], P(None, 'grp', 'gy'), may hold values from -2 to 2
- airflow_surface_forcing: float32 [2, 256, 1024], P(None, 'grp', 'gy'), may hold values from -3 to 3
- glacial_velocity_sigma: float32 [5, 256, 1024], P(None, 'grp', 'gy'), may hold values from -3 to 3
- category_coverage: float32 [5, 256, 1024], P(None, 'grp', 'gy'), may hold values from 0.17 to 0.2
- category_thickness: float32 [5, 256, 1024], P(None, 'grp', 'gy'), may hold values from 0.2 to 1
- seawater_indicator: int32 [256, 1024], P('grp', 'gy'), may hold values from 0 to 1
- dynamics_indicator: int32 [256, 1024], P('grp', 'gy'), may hold values from 0 to 1, as said below
- patch_home_position: int32 [16, 8], P('grp', 'gy'), may hold values from -1 to 3, as said below
Outputs:
- potential_warmth_updated: float32 [24, 256, 1024], P(None, 'grp', 'gy')
- saltiness_updated: float32 [24, 256, 1024], P(None, 'grp', 'gy')
- coupled_surface_velocity: float32 [2, 256, 1024], P(None, 'grp', 'gy')
- glacial_patch_update: float32 [5, 256, 1024], P(None, 'grp', 'gy')
The draws below stay inside these ranges and needn't reach their ends.
Inputs may be any that keep to these rules, and one draw needn't show every extreme that they name: For a block with ice, patch_home_position = d * 2 + p: it goes to slot p from its tile of the device with the same grp index and gy index d; no two blocks of one tile share a value; the first tile row holds 4 blocks with ice in every draw. `dynamics_indicator`: 1 only at cells with seawater_indicator 1 inside blocks whose patch_home_position is not negative.
All inputs are finite; a program needn't handle non-finite values.
Results may differ from the reference program's by a relative error of at most 0.0003.
Values sent between devices are 32-bit elements; how exact they have to be, the bound alone decides.
A program may use at most 64 MiB of HBM per device.

```python
import math
import jax
import jax.numpy as jnp
from jax import lax

CX = 16
BY = 128
NB = 4
NSUB = 4
VERTICAL_COUNT = 24
NCAT = 5
PAIR = 2
GRID_EAST_COUNT = 256
GRID_NORTH_COUNT = 1024
NBY = 8
N_GRP = 16
N_GY = 2


def routing_tables(key):
    cell_key = jax.random.fold_in(key, 11)
    block_key = jax.random.fold_in(key, 12)
    rotate_key = jax.random.fold_in(key, 13)
    speck_key = jax.random.fold_in(key, 14)
    seawater_points = (jax.random.randint(cell_key, (GRID_EAST_COUNT, GRID_NORTH_COUNT), 0, 8) != 0).astype(jnp.int32)
    block_row = jnp.arange(NBY, dtype=jnp.int32)
    polar_rows = (block_row < NB) | (block_row >= NBY - NB // 2)
    random_ice = jax.random.randint(block_key, (N_GRP, NBY), 0, 3) == 0
    iced_blocks = (polar_rows[None, :] | random_ice).astype(jnp.int32)
    tile_blocks = iced_blocks.reshape(N_GRP, N_GY, NB)
    order_rank = jnp.cumsum(tile_blocks, axis=2) - tile_blocks
    rotation = jax.random.randint(rotate_key, (N_GRP, N_GY, 1), 0, N_GY)
    slot_value = (rotation + order_rank) % N_GY * PAIR + order_rank // N_GY
    patch_home_position = jnp.where(tile_blocks > 0, slot_value, -1).reshape(N_GRP, NBY).astype(jnp.int32)
    cell_iced = jnp.repeat(jnp.repeat(iced_blocks, CX, axis=0), BY, axis=1)
    speckles = (jax.random.randint(speck_key, (GRID_EAST_COUNT, GRID_NORTH_COUNT), 0, 4) != 0).astype(jnp.int32)
    ice_cells = seawater_points * cell_iced * speckles
    return (seawater_points, ice_cells, patch_home_position)


def draw_seawater_indicator(key, part):
    return routing_tables(key)[0]


def draw_dynamics_indicator(key, part):
    return routing_tables(key)[1]


def draw_patch_home_position(key, part):
    return routing_tables(key)[2]


def block_scale(rng, shape, shards, least, high):
    gain = 1.0
    for position, shards_of in shards:
        steps = jax.random.uniform(jax.random.fold_in(jax.random.fold_in(rng, 6), position), (shards_of,), jnp.float32, least / len(shards), high / len(shards))
        gain = gain * jnp.repeat(jnp.exp(steps), shape[position] // shards_of).reshape((-1,) + (1,) * (len(shape) - 1 - position))
    return gain


def normal_values(own_key, shape, scale, bound, pieces=(), kind=jnp.bfloat16):
    array = scale * jax.random.normal(own_key, shape, jnp.float32)
    if pieces:
        array = array * block_scale(own_key, shape, pieces, -0.22, 0.18)
    return jnp.clip(array, -bound, bound).astype(kind)


def setup_inputs(seed: int = 0) -> dict:
    key_of = jax.random.split(jax.random.key(seed), 11)
    potential_warmth = jnp.clip(-2.0 + 6.0 * jax.random.uniform(key_of[0], (VERTICAL_COUNT, GRID_EAST_COUNT, GRID_NORTH_COUNT), jnp.float32) ** block_scale(key_of[0], (VERTICAL_COUNT, GRID_EAST_COUNT, GRID_NORTH_COUNT), ((1, 16), (2, 2)), -0.2, 0.2), -2.0, 4.0)
    saltiness_anomaly = normal_values(key_of[1], (VERTICAL_COUNT, GRID_EAST_COUNT, GRID_NORTH_COUNT), 1.0, 6.0, ((1, 16), (2, 2)), jnp.float32)
    seawater_velocity = normal_values(key_of[2], (2, GRID_EAST_COUNT, GRID_NORTH_COUNT), 0.3, 2.0, ((1, 16), (2, 2)), jnp.float32)
    airflow_surface_forcing = normal_values(key_of[3], (2, GRID_EAST_COUNT, GRID_NORTH_COUNT), 0.5, 3.0, ((1, 16), (2, 2)), jnp.float32)
    glacial_velocity_sigma = normal_values(key_of[4], (5, GRID_EAST_COUNT, GRID_NORTH_COUNT), 0.5, 3.0, ((1, 16), (2, 2)), jnp.float32)
    category_coverage = jnp.clip(0.17 + 0.030000001 * jax.random.uniform(key_of[5], (NCAT, GRID_EAST_COUNT, GRID_NORTH_COUNT), jnp.float32) ** block_scale(key_of[5], (NCAT, GRID_EAST_COUNT, GRID_NORTH_COUNT), ((1, 16), (2, 2)), -0.2, 0.2), 0.17, 0.2)
    category_thickness = jnp.clip(jnp.exp(math.log(1.0) - 1.609438 * jax.random.uniform(key_of[6], (NCAT, GRID_EAST_COUNT, GRID_NORTH_COUNT), jnp.float32) ** block_scale(key_of[6], (NCAT, GRID_EAST_COUNT, GRID_NORTH_COUNT), ((1, 16), (2, 2)), -0.2, 0.2)), 0.2, 1.0)
    seawater_indicator = draw_seawater_indicator(jax.random.fold_in(key_of[10], 71), 0)
    dynamics_indicator = draw_dynamics_indicator(jax.random.fold_in(key_of[10], 71), 0)
    patch_home_position = draw_patch_home_position(jax.random.fold_in(key_of[10], 71), 0)
    return dict(potential_warmth=potential_warmth, saltiness_anomaly=saltiness_anomaly, seawater_velocity=seawater_velocity, airflow_surface_forcing=airflow_surface_forcing, glacial_velocity_sigma=glacial_velocity_sigma, category_coverage=category_coverage, category_thickness=category_thickness, seawater_indicator=seawater_indicator, dynamics_indicator=dynamics_indicator, patch_home_position=patch_home_position)


DIFFUSIVITY = 0.2
STRENGTH_COEF = 20.0
MIN_MASS = 0.5
RELAX_RATE = 0.5
ECCENTRIC = 4.0
DELTA_FLOOR = 0.0025
SPEED_FLOOR = 0.01
CORIOLIS = 0.5
HEAT_COEF = 4.0
THIN_LIMIT = 0.1
FREEZING = -1.8
WARMTH_FACTOR = 0.05
STRESS_SCALE = 0.5

def east_of(field, offset):
    return jnp.roll(field, -offset, axis=-2)

def north_of(field, offset):
    border = jnp.zeros_like(field[..., :1])
    if offset > 0:
        return jnp.concatenate([field[..., 1:], border], axis=-1)
    return jnp.concatenate([border, field[..., :-1]], axis=-1)

def evp_subcycles(vel_u, vel_v, sig_one, sig_two, sig_shear, cur_u, cur_v, concentration, thickness, wind_u, wind_v, glacial_indicator):
    strength = thickness * jnp.exp(-STRENGTH_COEF * (1.0 - concentration))
    ice_mass = thickness + MIN_MASS
    for subcycle in range(NSUB):
        u_east = east_of(vel_u, 1) - vel_u
        v_north = north_of(vel_v, 1) - vel_v
        u_north = north_of(vel_u, 1) - vel_u
        v_east = east_of(vel_v, 1) - vel_v
        divergence = u_east + v_north
        tension = u_east - v_north
        shear_rate = u_north + v_east
        deform_rate = jnp.sqrt(divergence * divergence + (tension * tension + shear_rate * shear_rate) / ECCENTRIC + DELTA_FLOOR)
        viscous = strength / deform_rate
        sig_one = glacial_indicator * (sig_one + RELAX_RATE * (viscous * divergence - strength)) / (1.0 + RELAX_RATE)
        sig_two = glacial_indicator * (sig_two + RELAX_RATE * viscous * tension / ECCENTRIC) / (1.0 + RELAX_RATE)
        sig_shear = glacial_indicator * (sig_shear + RELAX_RATE * viscous * shear_rate / ECCENTRIC) / (1.0 + RELAX_RATE)
        back_one_x = sig_one - east_of(sig_one, -1)
        back_two_x = sig_two - east_of(sig_two, -1)
        back_one_y = sig_one - north_of(sig_one, -1)
        back_two_y = sig_two - north_of(sig_two, -1)
        force_u = 0.5 * (back_one_x + back_two_x) + (sig_shear - north_of(sig_shear, -1))
        force_v = 0.5 * (back_one_y - back_two_y) + (sig_shear - east_of(sig_shear, -1))
        rel_speed = jnp.sqrt((cur_u - vel_u) ** 2 + (cur_v - vel_v) ** 2 + SPEED_FLOOR)
        water_coef = concentration * rel_speed
        implicit = ice_mass + water_coef
        new_u = glacial_indicator * (ice_mass * vel_u + force_u + wind_u + water_coef * cur_u + CORIOLIS * ice_mass * vel_v) / implicit
        new_v = glacial_indicator * (ice_mass * vel_v + force_v + wind_v + water_coef * cur_v - CORIOLIS * ice_mass * vel_u) / implicit
        vel_u, vel_v = (new_u, new_v)
    rel_speed = jnp.sqrt((cur_u - vel_u) ** 2 + (cur_v - vel_v) ** 2 + SPEED_FLOOR)
    water_coef = concentration * rel_speed
    stress_u = glacial_indicator * water_coef * (vel_u - cur_u)
    stress_v = glacial_indicator * water_coef * (vel_v - cur_v)
    return ((vel_u, vel_v, sig_one, sig_two, sig_shear), (stress_u, stress_v))

def seabed_exchange(surface_temp, category_coverage, category_thickness, glacial_indicator, cat_axis):
    per_cat = HEAT_COEF * category_coverage * category_coverage / (category_thickness + THIN_LIMIT * category_coverage)
    return glacial_indicator * (surface_temp - FREEZING) * lax.optimization_barrier(jnp.sum(per_cat, axis=cat_axis))

def reference(potential_warmth, saltiness_anomaly, seawater_velocity, airflow_surface_forcing, glacial_velocity_sigma, category_coverage, category_thickness, seawater_indicator, dynamics_indicator, patch_home_position):
    seawater_points = seawater_indicator.astype(jnp.float32)
    glacial_indicator = dynamics_indicator.astype(jnp.float32)
    concentration = lax.optimization_barrier(jnp.sum(category_coverage, axis=0))
    thickness = lax.optimization_barrier(jnp.sum(category_thickness, axis=0))

    def diffuse_quantity(field):
        inflow = jnp.zeros_like(field)
        for near_field, near_wet in ((east_of(field, 1), east_of(seawater_points, 1)), (east_of(field, -1), east_of(seawater_points, -1)), (north_of(field, 1), north_of(seawater_points, 1)), (north_of(field, -1), north_of(seawater_points, -1))):
            inflow = inflow + near_wet * (near_field - field)
        return field + DIFFUSIVITY * seawater_points * inflow
    state, stress = evp_subcycles(glacial_velocity_sigma[0], glacial_velocity_sigma[1], glacial_velocity_sigma[2], glacial_velocity_sigma[3], glacial_velocity_sigma[4], seawater_velocity[0], seawater_velocity[1], concentration, thickness, airflow_surface_forcing[0], airflow_surface_forcing[1], glacial_indicator)
    heat_exchange = seabed_exchange(potential_warmth[0], category_coverage, category_thickness, glacial_indicator, 0)
    potential_warmth_updated = diffuse_quantity(potential_warmth)
    potential_warmth_updated = potential_warmth_updated.at[0].add(-WARMTH_FACTOR * seawater_points * heat_exchange)
    saltiness_updated = diffuse_quantity(saltiness_anomaly)
    coupled_surface_velocity = seawater_points * (seawater_velocity + STRESS_SCALE * jnp.stack(stress))
    ice_new = jnp.stack(state)
    blocks = ice_new.reshape(5, N_GRP, CX, NBY, BY).transpose(1, 3, 0, 2, 4)
    tile_row = (jnp.arange(NBY, dtype=jnp.int32) // NB).astype(jnp.int32)
    target = jnp.where(patch_home_position >= 0, patch_home_position // PAIR * NB + tile_row[None, :] * PAIR + patch_home_position % PAIR, NBY).astype(jnp.int32)
    grp_rows = jnp.arange(N_GRP, dtype=jnp.int32)[:, None]
    placed = jnp.zeros((N_GRP, NBY + 1, 5, CX, BY), jnp.float32)
    placed = placed.at[grp_rows, target].set(blocks)
    glacial_patch_update = placed[:, :NBY].transpose(2, 0, 3, 1, 4).reshape(5, GRID_EAST_COUNT, GRID_NORTH_COUNT)
    return (potential_warmth_updated, saltiness_updated, coupled_surface_velocity, glacial_patch_update)
```

```python
import functools

import jax
import jax.numpy as jnp
from jax import lax
from jax.experimental import pallas as pl
from jax.experimental.pallas import tpu as pltpu
from jax.sharding import PartitionSpec as P

NSUB = 4
DIFFUSIVITY = 0.2
STRENGTH_COEF = 20.0
MIN_MASS = 0.5
RELAX_RATE = 0.5
ECCENTRIC = 4.0
DELTA_FLOOR = 0.0025
SPEED_FLOOR = 0.01
CORIOLIS = 0.5
HEAT_COEF = 4.0
THIN_LIMIT = 0.1
FREEZING = -1.8
WARMTH_FACTOR = 0.05
STRESS_SCALE = 0.5

LANES = 128
PLANES = 12
A_PLANE, H_PLANE, ICY_PLANE = 9, 10, 11


def shift(field, offset, axis):
    size = field.shape[axis]
    return pltpu.roll(field, (-offset) % size, axis)


def kernel(
    n_grp, n_gy, levels, rows, cols, nblock,
    home, pw, sa, sv, af, gvs, cc, ct, si, di,
    pw_out, sa_out, vel_out, glac_out,
    win, ccv, ctv, siv, div_, pwv, sav, pwo, sao, coef, cvel, heat,
    icy_rows, wet_rows, halo_rows,
    pack_hi, pack_lo, tpack_hi, tpack_lo, got_hi, got_lo, tgot_hi, tgot_lo,
    mine, picks,
    in_sem, out_sem, row_send, row_recv, col_send, col_recv, patch_send, patch_recv,
):
    g = lax.axis_index("grp")
    y = lax.axis_index("gy")
    east = lax.rem(g + 1, n_grp)
    west = lax.rem(g + n_grp - 1, n_grp)
    has_up = y < n_gy - 1
    has_dn = y > 0
    ext = rows + 2 * NSUB
    block_len = cols // nblock
    pair = nblock // n_gy

    center = (slice(0, rows), slice(0, cols))
    loads = [
        pltpu.make_async_copy(src, dst, in_sem.at[i])
        for i, (src, dst) in enumerate(
            (
                (cc, ccv),
                (ct, ctv),
                (di, div_),
                (si, siv),
                (gvs, win.at[0:5, 0:rows, 0:cols]),
                (sv, win.at[5:7, 0:rows, 0:cols]),
                (af, win.at[7:9, 0:rows, 0:cols]),
                (pw, pwv),
                (sa, sav),
            )
        )
    ]
    for load in loads:
        load.start()

    barrier = pltpu.get_barrier_semaphore()

    def greet(gg, yy):
        pl.semaphore_signal(
            barrier, inc=1, device_id={"grp": gg, "gy": yy},
            device_id_type=pl.DeviceIdType.MESH,
        )

    greet(east, y)
    greet(west, y)
    for k in range(1, n_gy):
        greet(g, lax.rem(y + k, n_gy))

    @pl.when(has_up)
    def _():
        greet(east, y + 1)
        greet(west, y + 1)

    @pl.when(has_dn)
    def _():
        greet(east, y - 1)
        greet(west, y - 1)

    both = jnp.where(has_up, 2, 0) + jnp.where(has_dn, 2, 0)

    for load in loads[:4]:
        load.wait()
    win[A_PLANE, 0:rows, 0:cols] = jnp.sum(ccv[...], axis=0)
    win[H_PLANE, 0:rows, 0:cols] = jnp.sum(ctv[...], axis=0)
    win[ICY_PLANE, 0:rows, 0:cols] = div_[...].astype(jnp.float32)
    wet = siv[...].astype(jnp.float32)
    for load in loads[4:7]:
        load.wait()

    lane16 = lax.broadcasted_iota(jnp.int32, (rows, LANES), 1)

    def pack(entries):
        out = jnp.zeros((rows, LANES), jnp.float32)
        for tile, first, place, width in entries:
            moved = pltpu.roll(tile, (place - first) % LANES, 1)
            out = jnp.where((lane16 >= place) & (lane16 < place + width), moved, out)
        return out

    wet_lane = PLANES * NSUB
    hi = slice(cols - LANES, cols)
    lo = slice(0, LANES)
    pack_hi[...] = pack(
        [(win[p, 0:rows, hi], LANES - NSUB, NSUB * p, NSUB) for p in range(PLANES)]
        + [(wet[:, hi], LANES - 1, wet_lane, 1)]
    )
    pack_lo[...] = pack(
        [(win[p, 0:rows, lo], 0, NSUB * p, NSUB) for p in range(PLANES)]
        + [(wet[:, lo], 0, wet_lane, 1)]
    )

    pl.semaphore_wait(barrier, 1 + n_gy + both)

    def remote(src, dst, send, recv, gg, yy):
        return pltpu.make_async_remote_copy(
            src_ref=src, dst_ref=dst, send_sem=send, recv_sem=recv,
            device_id={"grp": gg, "gy": yy}, device_id_type=pl.DeviceIdType.MESH,
        )

    count = 0
    ice_rows, tracer_rows = [], []
    for to, first, at, edge, sub in (
        (west, 0, rows, 0, 7),
        (east, rows - NSUB, rows + NSUB, rows - 1, 0),
    ):
        src_rows = slice(first, first + NSUB)
        dst_rows = slice(at, at + NSUB)
        ice_pairs = (
            (gvs.at[:, src_rows, :], win.at[0:5, dst_rows, 0:cols]),
            (sv.at[:, src_rows, :], win.at[5:7, dst_rows, 0:cols]),
            (af.at[:, src_rows, :], win.at[7:9, dst_rows, 0:cols]),
            (win.at[A_PLANE : H_PLANE + 1, src_rows, 0:cols],
             win.at[A_PLANE : H_PLANE + 1, dst_rows, 0:cols]),
            (di.at[src_rows, :], icy_rows.at[at - rows : at - rows + NSUB, :]),
        )
        tracer_pairs = (
            (si.at[edge : edge + 1, :], wet_rows.at[sub : sub + 1, :]),
            (pw.at[:, edge : edge + 1, :], halo_rows.at[0:levels, sub : sub + 1, :]),
            (sa.at[:, edge : edge + 1, :], halo_rows.at[levels : 2 * levels, sub : sub + 1, :]),
        )
        for pairs, keep in ((ice_pairs, ice_rows), (tracer_pairs, tracer_rows)):
            for src, dst in pairs:
                keep.append(remote(src, dst, row_send.at[count], row_recv.at[count], to, y))
                count += 1
    for copy in ice_rows:
        copy.start()

    ice_up = [
        remote(pack_hi, got_lo.at[0:rows, :], col_send.at[0], col_recv.at[0], g, y + 1),
        remote(pack_hi.at[0:NSUB, :], got_lo.at[rows : rows + NSUB, :],
               col_send.at[1], col_recv.at[1], west, y + 1),
        remote(pack_hi.at[rows - NSUB : rows, :], got_lo.at[rows + NSUB : ext, :],
               col_send.at[2], col_recv.at[2], east, y + 1),
    ]
    ice_dn = [
        remote(pack_lo, got_hi.at[0:rows, :], col_send.at[3], col_recv.at[3], g, y - 1),
        remote(pack_lo.at[0:NSUB, :], got_hi.at[rows : rows + NSUB, :],
               col_send.at[4], col_recv.at[4], west, y - 1),
        remote(pack_lo.at[rows - NSUB : rows, :], got_hi.at[rows + NSUB : ext, :],
               col_send.at[5], col_recv.at[5], east, y - 1),
    ]
    tr_up = remote(tpack_hi, tgot_lo, col_send.at[6], col_recv.at[6], g, y + 1)
    tr_dn = remote(tpack_lo, tgot_hi, col_send.at[7], col_recv.at[7], g, y - 1)

    @pl.when(has_up)
    def _():
        for copy in ice_up:
            copy.start()

    @pl.when(has_dn)
    def _():
        for copy in ice_dn:
            copy.start()

    for copy in tracer_rows:
        copy.start()

    for load in loads[7:]:
        load.wait()
    for out, cut, first in ((tpack_hi, hi, LANES - 1), (tpack_lo, lo, 0)):
        out[...] = pack(
            [(pwv[l, :, cut], first, l, 1) for l in range(levels)]
            + [(sav[l, :, cut], first, levels + l, 1) for l in range(levels)]
        )

    @pl.when(has_up)
    def _():
        tr_up.start()

    @pl.when(has_dn)
    def _():
        tr_dn.start()

    coverage = ccv[...]
    per_cat = HEAT_COEF * coverage * coverage / (ctv[...] + THIN_LIMIT * coverage)
    heat[...] = (
        (WARMTH_FACTOR * wet)
        * (win[ICY_PLANE, 0:rows, 0:cols] * (pwv[0] - FREEZING) * jnp.sum(per_cat, axis=0))
    )

    @pl.when(jnp.logical_not(has_up))
    def _():
        got_hi[...] = jnp.zeros_like(got_hi)
        tgot_hi[...] = jnp.zeros_like(tgot_hi)

    @pl.when(jnp.logical_not(has_dn))
    def _():
        got_lo[...] = jnp.zeros_like(got_lo)
        tgot_lo[...] = jnp.zeros_like(tgot_lo)

    for copy in ice_rows:
        copy.wait_recv()

    @pl.when(has_up)
    def _():
        for copy in ice_dn:
            copy.wait_recv()

    @pl.when(has_dn)
    def _():
        for copy in ice_up:
            copy.wait_recv()

    win[ICY_PLANE, rows:ext, 0:cols] = icy_rows[...].astype(jnp.float32)
    lane24 = lax.broadcasted_iota(jnp.int32, (ext, LANES), 1)
    from_hi, from_lo = got_hi[...], got_lo[...]
    for p in range(PLANES):
        high = pltpu.roll(from_hi, (-NSUB * p) % LANES, 1)
        low = pltpu.roll(from_lo, (LANES - NSUB - NSUB * p) % LANES, 1)
        win[p, :, cols : cols + LANES] = jnp.where(
            lane24 < NSUB, high, jnp.where(lane24 >= LANES - NSUB, low, 0.0)
        )

    vel_u, vel_v = win[0], win[1]
    sig_one, sig_two, sig_shear = win[2], win[3], win[4]
    cur_u, cur_v, wind_u, wind_v = win[5], win[6], win[7], win[8]
    conc, thick, icy = win[A_PLANE], win[H_PLANE], win[ICY_PLANE]
    strength = thick * jnp.exp(-STRENGTH_COEF * (1.0 - conc))
    mass = thick + MIN_MASS
    keep = icy * (1.0 / (1.0 + RELAX_RATE))
    push = keep * strength * RELAX_RATE
    push_dev = push * (1.0 / ECCENTRIC)

    def drag(u, v):
        square = (cur_u - u) ** 2 + (cur_v - v) ** 2 + SPEED_FLOOR
        return conc * (square * lax.rsqrt(square))

    for _ in range(NSUB):
        u_east = shift(vel_u, 1, 0) - vel_u
        v_north = shift(vel_v, 1, 1) - vel_v
        u_north = shift(vel_u, 1, 1) - vel_u
        v_east = shift(vel_v, 1, 0) - vel_v
        diverge = u_east + v_north
        tension = u_east - v_north
        shear = u_north + v_east
        inverse = lax.rsqrt(
            diverge * diverge
            + (tension * tension + shear * shear) * (1.0 / ECCENTRIC)
            + DELTA_FLOOR
        )
        sig_one = keep * sig_one + push * (diverge * inverse - 1.0)
        scaled = push_dev * inverse
        sig_two = keep * sig_two + scaled * tension
        sig_shear = keep * sig_shear + scaled * shear
        total = sig_one + sig_two
        differ = sig_one - sig_two
        force_u = 0.5 * (total - shift(total, -1, 0)) + (sig_shear - shift(sig_shear, -1, 1))
        force_v = 0.5 * (differ - shift(differ, -1, 1)) + (sig_shear - shift(sig_shear, -1, 0))
        water = drag(vel_u, vel_v)
        scale = icy / (mass + water)
        turn_u = (CORIOLIS * mass) * vel_v
        turn_v = (CORIOLIS * mass) * vel_u
        new_u = (mass * vel_u + force_u + wind_u + water * cur_u + turn_u) * scale
        new_v = (mass * vel_v + force_v + wind_v + water * cur_v - turn_v) * scale
        vel_u, vel_v = new_u, new_v

    state = [f[0:rows, 0:cols] for f in (vel_u, vel_v, sig_one, sig_two, sig_shear)]

    homes = [home[0, b] for b in range(nblock)]

    def choose(slot, field):
        out = jnp.zeros((rows, block_len), jnp.float32)
        for b in range(nblock):
            out = jnp.where(homes[b] == slot, field[:, b * block_len : (b + 1) * block_len], out)
        return out

    span = pair * block_len
    place = pl.ds(pl.multiple_of(y * span, LANES), span)
    patches = []
    for k in range(1, n_gy):
        peer = lax.rem(y + k, n_gy)
        for f in range(5):
            for p in range(pair):
                picks[k - 1, f, :, p * block_len : (p + 1) * block_len] = choose(
                    peer * pair + p, state[f]
                )
        copy = remote(
            picks.at[k - 1], glac_out.at[:, :, place],
            patch_send.at[k - 1], patch_recv.at[k - 1], g, peer,
        )
        copy.start()
        patches.append(copy)
    for f in range(5):
        for p in range(pair):
            mine[f, :, p * block_len : (p + 1) * block_len] = choose(y * pair + p, state[f])
    outs = [pltpu.make_async_copy(mine, glac_out.at[:, :, place], out_sem.at[0])]
    outs[0].start()

    wide_u = icy * drag(vel_u, vel_v)
    tau_u = (wide_u * (vel_u - cur_u))[0:rows, 0:cols]
    tau_v = (wide_u * (vel_v - cur_v))[0:rows, 0:cols]
    cvel[0] = wet * (cur_u[0:rows, 0:cols] + STRESS_SCALE * tau_u)
    cvel[1] = wet * (cur_v[0:rows, 0:cols] + STRESS_SCALE * tau_v)
    outs.append(pltpu.make_async_copy(cvel, vel_out, out_sem.at[1]))
    outs[1].start()

    for copy in tracer_rows:
        copy.wait_recv()

    @pl.when(has_up)
    def _():
        tr_dn.wait_recv()

    @pl.when(has_dn)
    def _():
        tr_up.wait_recv()

    row = lax.broadcasted_iota(jnp.int32, (rows, cols), 0)
    lane = lax.broadcasted_iota(jnp.int32, (rows, cols), 1)
    reps = cols // LANES

    def neighbours(field, edge_rows, high, low):
        edge = jnp.concatenate([edge_rows] * (rows // 8), axis=0)
        high = jnp.concatenate([high] * reps, axis=1)
        low = jnp.concatenate([low] * reps, axis=1)
        return (
            jnp.where(row == rows - 1, edge, shift(field, 1, 0)),
            jnp.where(row == 0, edge, shift(field, -1, 0)),
            jnp.where(lane == cols - 1, high, shift(field, 1, 1)),
            jnp.where(lane == 0, low, shift(field, -1, 1)),
        )

    near = neighbours(
        wet,
        wet_rows[...].astype(jnp.float32),
        pltpu.roll(got_hi[0:rows, :], (LANES - 1 - wet_lane) % LANES, 1),
        pltpu.roll(got_lo[0:rows, :], (-wet_lane) % LANES, 1),
    )
    rate = DIFFUSIVITY * wet
    weights = [rate * n for n in near]
    for i in range(4):
        coef[i] = weights[i]
    coef[4] = 1.0 - (weights[0] + weights[1] + weights[2] + weights[3])

    chunks = 4
    step = levels // chunks
    thi, tlo = tgot_hi[...], tgot_lo[...]
    sem = 2
    for c in range(chunks):
        for src, dst, base in ((pwv, pwo, 0), (sav, sao, levels)):
            for l in range(c * step, (c + 1) * step):
                at = base + l
                field = src[l]
                sides = neighbours(
                    field,
                    halo_rows[at],
                    pltpu.roll(thi, (LANES - 1 - at) % LANES, 1),
                    pltpu.roll(tlo, (-at) % LANES, 1),
                )
                mixed = coef[4] * field
                for i in range(4):
                    mixed = mixed + coef[i] * sides[i]
                if at == 0:
                    mixed = mixed - heat[...]
                dst[l] = mixed
        for src, dst in ((pwo, pw_out), (sao, sa_out)):
            cut = slice(c * step, (c + 1) * step)
            copy = pltpu.make_async_copy(src.at[cut], dst.at[cut], out_sem.at[sem])
            copy.start()
            outs.append(copy)
            sem += 1

    for copy in ice_rows + tracer_rows:
        copy.wait_send()

    @pl.when(has_up)
    def _():
        for copy in ice_up + [tr_up]:
            copy.wait_send()

    @pl.when(has_dn)
    def _():
        for copy in ice_dn + [tr_dn]:
            copy.wait_send()

    for copy in patches:
        copy.wait()
    for copy in outs:
        copy.wait()


def per_device(
    n_grp, n_gy, pw, sa, sv, af, gvs, cc, ct, si, di, home
):
    levels, rows, cols = pw.shape
    nblock = home.shape[1]
    block_len = cols // nblock
    pair = nblock // n_gy
    ext = rows + 2 * NSUB
    f32, i32 = jnp.float32, jnp.int32
    any_space = pl.BlockSpec(memory_space=pl.ANY)
    tile = lambda *shape: pltpu.VMEM(shape, f32)
    return pl.pallas_call(
        functools.partial(kernel, n_grp, n_gy, levels, rows, cols, nblock),
        out_shape=(
            jax.ShapeDtypeStruct(pw.shape, f32),
            jax.ShapeDtypeStruct(sa.shape, f32),
            jax.ShapeDtypeStruct(sv.shape, f32),
            jax.ShapeDtypeStruct(gvs.shape, f32),
        ),
        in_specs=[pl.BlockSpec(memory_space=pltpu.SMEM)] + [any_space] * 9,
        out_specs=(any_space,) * 4,
        scratch_shapes=[
            tile(PLANES, ext, cols + LANES),
            tile(*cc.shape),
            tile(*ct.shape),
            pltpu.VMEM((rows, cols), i32),
            pltpu.VMEM((rows, cols), i32),
            tile(*pw.shape),
            tile(*sa.shape),
            tile(*pw.shape),
            tile(*sa.shape),
            tile(5, rows, cols),
            tile(2, rows, cols),
            tile(rows, cols),
            pltpu.VMEM((2 * NSUB, cols), i32),
            pltpu.VMEM((8, cols), i32),
            tile(2 * levels, 8, cols),
            tile(rows, LANES),
            tile(rows, LANES),
            tile(rows, LANES),
            tile(rows, LANES),
            tile(ext, LANES),
            tile(ext, LANES),
            tile(rows, LANES),
            tile(rows, LANES),
            tile(5, rows, pair * block_len),
            tile(max(n_gy - 1, 1), 5, rows, pair * block_len),
            pltpu.SemaphoreType.DMA((9,)),
            pltpu.SemaphoreType.DMA((10,)),
            pltpu.SemaphoreType.DMA((16,)),
            pltpu.SemaphoreType.DMA((16,)),
            pltpu.SemaphoreType.DMA((8,)),
            pltpu.SemaphoreType.DMA((8,)),
            pltpu.SemaphoreType.DMA((max(n_gy - 1, 1),)),
            pltpu.SemaphoreType.DMA((max(n_gy - 1, 1),)),
        ],
        compiler_params=pltpu.CompilerParams(collective_id=0, has_side_effects=True),
    )(home, pw, sa, sv, af, gvs, cc, ct, si, di)


def solution(mesh):
    field = P(None, "grp", "gy")
    flat = P("grp", "gy")
    return jax.shard_map(
        functools.partial(per_device, mesh.shape["grp"], mesh.shape["gy"]),
        mesh=mesh,
        in_specs=(field,) * 7 + (flat,) * 3,
        out_specs=(field,) * 4,
        check_vma=False,
    )
```

```python
import functools

import jax
import jax.numpy as jnp
from jax import lax
from jax.experimental import pallas as pl
from jax.experimental.pallas import tpu as pltpu
from jax.sharding import PartitionSpec as P

NSUB = 4
DIFFUSIVITY = 0.2
STRENGTH_COEF = 20.0
MIN_MASS = 0.5
RELAX_RATE = 0.5
ECCENTRIC = 4.0
DELTA_FLOOR = 0.0025
SPEED_FLOOR = 0.01
CORIOLIS = 0.5
HEAT_COEF = 4.0
THIN_LIMIT = 0.1
FREEZING = -1.8
WARMTH_FACTOR = 0.05
STRESS_SCALE = 0.5

LANES = 128
PLANES = 12
A_PLANE, H_PLANE, ICY_PLANE = 9, 10, 11


def shift(field, offset, axis):
    size = field.shape[axis]
    return pltpu.roll(field, (-offset) % size, axis)


def kernel(
    n_grp, n_gy, levels, rows, cols, nblock,
    home, pw, sa, sv, af, gvs, cc, ct, si, di,
    pwo, sao, cvel, glac_out,
    win, ccv, ctv, siv, div_, pwv, sav, coef, heat,
    icy_rows, wet_rows, halo_rows,
    pack_hi, pack_lo, tpack_hi, tpack_lo, got_hi, got_lo, tgot_hi, tgot_lo,
    picks,
    in_sem, row_send, row_recv, col_send, col_recv, patch_send, patch_recv,
):
    g = lax.axis_index("grp")
    y = lax.axis_index("gy")
    east = lax.rem(g + 1, n_grp)
    west = lax.rem(g + n_grp - 1, n_grp)
    has_up = y < n_gy - 1
    has_dn = y > 0
    ext = rows + 2 * NSUB
    block_len = cols // nblock
    pair = nblock // n_gy

    center = (slice(0, rows), slice(0, cols))
    loads = [
        pltpu.make_async_copy(src, dst, in_sem.at[i])
        for i, (src, dst) in enumerate(
            (
                (cc, ccv),
                (ct, ctv),
                (di, div_),
                (si, siv),
                (gvs, win.at[0:5, 0:rows, 0:cols]),
                (sv, win.at[5:7, 0:rows, 0:cols]),
                (af, win.at[7:9, 0:rows, 0:cols]),
                (pw, pwv),
                (sa, sav),
            )
        )
    ]
    for load in loads:
        load.start()

    barrier = pltpu.get_barrier_semaphore()

    def greet(gg, yy):
        pl.semaphore_signal(
            barrier, inc=1, device_id={"grp": gg, "gy": yy},
            device_id_type=pl.DeviceIdType.MESH,
        )

    greet(east, y)
    greet(west, y)
    for k in range(1, n_gy):
        greet(g, lax.rem(y + k, n_gy))

    @pl.when(has_up)
    def _():
        greet(east, y + 1)
        greet(west, y + 1)

    @pl.when(has_dn)
    def _():
        greet(east, y - 1)
        greet(west, y - 1)

    both = jnp.where(has_up, 2, 0) + jnp.where(has_dn, 2, 0)

    for load in loads[:4]:
        load.wait()
    win[A_PLANE, 0:rows, 0:cols] = jnp.sum(ccv[...], axis=0)
    win[H_PLANE, 0:rows, 0:cols] = jnp.sum(ctv[...], axis=0)
    win[ICY_PLANE, 0:rows, 0:cols] = div_[...].astype(jnp.float32)
    wet = siv[...].astype(jnp.float32)
    for load in loads[4:7]:
        load.wait()

    lane16 = lax.broadcasted_iota(jnp.int32, (rows, LANES), 1)

    def pack(entries):
        out = jnp.zeros((rows, LANES), jnp.float32)
        for tile, first, place, width in entries:
            moved = pltpu.roll(tile, (place - first) % LANES, 1)
            out = jnp.where((lane16 >= place) & (lane16 < place + width), moved, out)
        return out

    wet_lane = PLANES * NSUB
    hi = slice(cols - LANES, cols)
    lo = slice(0, LANES)
    pack_hi[...] = pack(
        [(win[p, 0:rows, hi], LANES - NSUB, NSUB * p, NSUB) for p in range(PLANES)]
        + [(wet[:, hi], LANES - 1, wet_lane, 1)]
    )
    pack_lo[...] = pack(
        [(win[p, 0:rows, lo], 0, NSUB * p, NSUB) for p in range(PLANES)]
        + [(wet[:, lo], 0, wet_lane, 1)]
    )

    pl.semaphore_wait(barrier, 1 + n_gy + both)

    def remote(src, dst, send, recv, gg, yy):
        return pltpu.make_async_remote_copy(
            src_ref=src, dst_ref=dst, send_sem=send, recv_sem=recv,
            device_id={"grp": gg, "gy": yy}, device_id_type=pl.DeviceIdType.MESH,
        )

    count = 0
    ice_rows, tracer_rows = [], []
    for to, first, at, edge, sub in (
        (west, 0, rows, 0, 7),
        (east, rows - NSUB, rows + NSUB, rows - 1, 0),
    ):
        src_rows = slice(first, first + NSUB)
        dst_rows = slice(at, at + NSUB)
        ice_pairs = (
            (gvs.at[:, src_rows, :], win.at[0:5, dst_rows, 0:cols]),
            (sv.at[:, src_rows, :], win.at[5:7, dst_rows, 0:cols]),
            (af.at[:, src_rows, :], win.at[7:9, dst_rows, 0:cols]),
            (win.at[A_PLANE : H_PLANE + 1, src_rows, 0:cols],
             win.at[A_PLANE : H_PLANE + 1, dst_rows, 0:cols]),
            (di.at[src_rows, :], icy_rows.at[at - rows : at - rows + NSUB, :]),
        )
        tracer_pairs = (
            (si.at[edge : edge + 1, :], wet_rows.at[sub : sub + 1, :]),
            (pw.at[:, edge : edge + 1, :], halo_rows.at[0:levels, sub : sub + 1, :]),
            (sa.at[:, edge : edge + 1, :], halo_rows.at[levels : 2 * levels, sub : sub + 1, :]),
        )
        for pairs, keep in ((ice_pairs, ice_rows), (tracer_pairs, tracer_rows)):
            for src, dst in pairs:
                keep.append(remote(src, dst, row_send.at[count], row_recv.at[count], to, y))
                count += 1
    for copy in ice_rows:
        copy.start()

    ice_up = [
        remote(pack_hi, got_lo.at[0:rows, :], col_send.at[0], col_recv.at[0], g, y + 1),
        remote(pack_hi.at[0:NSUB, :], got_lo.at[rows : rows + NSUB, :],
               col_send.at[1], col_recv.at[1], west, y + 1),
        remote(pack_hi.at[rows - NSUB : rows, :], got_lo.at[rows + NSUB : ext, :],
               col_send.at[2], col_recv.at[2], east, y + 1),
    ]
    ice_dn = [
        remote(pack_lo, got_hi.at[0:rows, :], col_send.at[3], col_recv.at[3], g, y - 1),
        remote(pack_lo.at[0:NSUB, :], got_hi.at[rows : rows + NSUB, :],
               col_send.at[4], col_recv.at[4], west, y - 1),
        remote(pack_lo.at[rows - NSUB : rows, :], got_hi.at[rows + NSUB : ext, :],
               col_send.at[5], col_recv.at[5], east, y - 1),
    ]
    tr_up = remote(tpack_hi, tgot_lo, col_send.at[6], col_recv.at[6], g, y + 1)
    tr_dn = remote(tpack_lo, tgot_hi, col_send.at[7], col_recv.at[7], g, y - 1)

    @pl.when(has_up)
    def _():
        for copy in ice_up:
            copy.start()

    @pl.when(has_dn)
    def _():
        for copy in ice_dn:
            copy.start()

    for copy in tracer_rows:
        copy.start()

    for load in loads[7:]:
        load.wait()
    for out, cut, first in ((tpack_hi, hi, LANES - 1), (tpack_lo, lo, 0)):
        out[...] = pack(
            [(pwv[l, :, cut], first, l, 1) for l in range(levels)]
            + [(sav[l, :, cut], first, levels + l, 1) for l in range(levels)]
        )

    @pl.when(has_up)
    def _():
        tr_up.start()

    @pl.when(has_dn)
    def _():
        tr_dn.start()

    coverage = ccv[...]
    per_cat = HEAT_COEF * coverage * coverage / (ctv[...] + THIN_LIMIT * coverage)
    heat[...] = (
        (WARMTH_FACTOR * wet)
        * (win[ICY_PLANE, 0:rows, 0:cols] * (pwv[0] - FREEZING) * jnp.sum(per_cat, axis=0))
    )

    @pl.when(jnp.logical_not(has_up))
    def _():
        got_hi[...] = jnp.zeros_like(got_hi)
        tgot_hi[...] = jnp.zeros_like(tgot_hi)

    @pl.when(jnp.logical_not(has_dn))
    def _():
        got_lo[...] = jnp.zeros_like(got_lo)
        tgot_lo[...] = jnp.zeros_like(tgot_lo)

    for copy in ice_rows:
        copy.wait_recv()

    @pl.when(has_up)
    def _():
        for copy in ice_dn:
            copy.wait_recv()

    @pl.when(has_dn)
    def _():
        for copy in ice_up:
            copy.wait_recv()

    win[ICY_PLANE, rows:ext, 0:cols] = icy_rows[...].astype(jnp.float32)
    lane24 = lax.broadcasted_iota(jnp.int32, (ext, LANES), 1)
    from_hi, from_lo = got_hi[...], got_lo[...]
    for p in range(PLANES):
        high = pltpu.roll(from_hi, (-NSUB * p) % LANES, 1)
        low = pltpu.roll(from_lo, (LANES - NSUB - NSUB * p) % LANES, 1)
        win[p, :, cols : cols + LANES] = jnp.where(
            lane24 < NSUB, high, jnp.where(lane24 >= LANES - NSUB, low, 0.0)
        )

    vel_u, vel_v = win[0], win[1]
    sig_one, sig_two, sig_shear = win[2], win[3], win[4]
    cur_u, cur_v, wind_u, wind_v = win[5], win[6], win[7], win[8]
    conc, thick, icy = win[A_PLANE], win[H_PLANE], win[ICY_PLANE]
    strength = thick * jnp.exp(-STRENGTH_COEF * (1.0 - conc))
    mass = thick + MIN_MASS
    keep = icy * (1.0 / (1.0 + RELAX_RATE))
    push = keep * strength * RELAX_RATE
    push_dev = push * (1.0 / ECCENTRIC)

    def drag(u, v):
        square = (cur_u - u) ** 2 + (cur_v - v) ** 2 + SPEED_FLOOR
        return conc * (square * lax.rsqrt(square))

    for _ in range(NSUB):
        u_east = shift(vel_u, 1, 0) - vel_u
        v_north = shift(vel_v, 1, 1) - vel_v
        u_north = shift(vel_u, 1, 1) - vel_u
        v_east = shift(vel_v, 1, 0) - vel_v
        diverge = u_east + v_north
        tension = u_east - v_north
        shear = u_north + v_east
        inverse = lax.rsqrt(
            diverge * diverge
            + (tension * tension + shear * shear) * (1.0 / ECCENTRIC)
            + DELTA_FLOOR
        )
        sig_one = keep * sig_one + push * (diverge * inverse - 1.0)
        scaled = push_dev * inverse
        sig_two = keep * sig_two + scaled * tension
        sig_shear = keep * sig_shear + scaled * shear
        total = sig_one + sig_two
        differ = sig_one - sig_two
        force_u = 0.5 * (total - shift(total, -1, 0)) + (sig_shear - shift(sig_shear, -1, 1))
        force_v = 0.5 * (differ - shift(differ, -1, 1)) + (sig_shear - shift(sig_shear, -1, 0))
        water = drag(vel_u, vel_v)
        scale = icy / (mass + water)
        turn_u = (CORIOLIS * mass) * vel_v
        turn_v = (CORIOLIS * mass) * vel_u
        new_u = (mass * vel_u + force_u + wind_u + water * cur_u + turn_u) * scale
        new_v = (mass * vel_v + force_v + wind_v + water * cur_v - turn_v) * scale
        vel_u, vel_v = new_u, new_v

    state = [f[0:rows, 0:cols] for f in (vel_u, vel_v, sig_one, sig_two, sig_shear)]

    homes = [home[0, b] for b in range(nblock)]

    def choose(slot, field):
        out = jnp.zeros((rows, block_len), jnp.float32)
        for b in range(nblock):
            out = jnp.where(homes[b] == slot, field[:, b * block_len : (b + 1) * block_len], out)
        return out

    span = pair * block_len
    place = pl.ds(pl.multiple_of(y * span, LANES), span)
    patches = []
    for k in range(1, n_gy):
        peer = lax.rem(y + k, n_gy)
        for f in range(5):
            for p in range(pair):
                picks[k - 1, f, :, p * block_len : (p + 1) * block_len] = choose(
                    peer * pair + p, state[f]
                )
        copy = remote(
            picks.at[k - 1], glac_out.at[:, :, place],
            patch_send.at[k - 1], patch_recv.at[k - 1], g, peer,
        )
        copy.start()
        patches.append(copy)
    for f in range(5):
        for p in range(pair):
            glac_out[f, :, pl.ds(pl.multiple_of(y * span + p * block_len, LANES), block_len)] = (
                choose(y * pair + p, state[f])
            )

    wide_u = icy * drag(vel_u, vel_v)
    tau_u = (wide_u * (vel_u - cur_u))[0:rows, 0:cols]
    tau_v = (wide_u * (vel_v - cur_v))[0:rows, 0:cols]
    cvel[0] = wet * (cur_u[0:rows, 0:cols] + STRESS_SCALE * tau_u)
    cvel[1] = wet * (cur_v[0:rows, 0:cols] + STRESS_SCALE * tau_v)

    for copy in tracer_rows:
        copy.wait_recv()

    @pl.when(has_up)
    def _():
        tr_dn.wait_recv()

    @pl.when(has_dn)
    def _():
        tr_up.wait_recv()

    row = lax.broadcasted_iota(jnp.int32, (rows, cols), 0)
    lane = lax.broadcasted_iota(jnp.int32, (rows, cols), 1)
    reps = cols // LANES

    def neighbours(field, edge_rows, high, low):
        edge = jnp.concatenate([edge_rows] * (rows // 8), axis=0)
        high = jnp.concatenate([high] * reps, axis=1)
        low = jnp.concatenate([low] * reps, axis=1)
        return (
            jnp.where(row == rows - 1, edge, shift(field, 1, 0)),
            jnp.where(row == 0, edge, shift(field, -1, 0)),
            jnp.where(lane == cols - 1, high, shift(field, 1, 1)),
            jnp.where(lane == 0, low, shift(field, -1, 1)),
        )

    near = neighbours(
        wet,
        wet_rows[...].astype(jnp.float32),
        pltpu.roll(got_hi[0:rows, :], (LANES - 1 - wet_lane) % LANES, 1),
        pltpu.roll(got_lo[0:rows, :], (-wet_lane) % LANES, 1),
    )
    rate = DIFFUSIVITY * wet
    weights = [rate * n for n in near]
    for i in range(4):
        coef[i] = weights[i]
    coef[4] = 1.0 - (weights[0] + weights[1] + weights[2] + weights[3])

    thi, tlo = tgot_hi[...], tgot_lo[...]
    for src, dst, base in ((pwv, pwo, 0), (sav, sao, levels)):
        for l in range(levels):
            at = base + l
            field = src[l]
            sides = neighbours(
                field,
                halo_rows[at],
                pltpu.roll(thi, (LANES - 1 - at) % LANES, 1),
                pltpu.roll(tlo, (-at) % LANES, 1),
            )
            mixed = coef[4] * field
            for i in range(4):
                mixed = mixed + coef[i] * sides[i]
            if at == 0:
                mixed = mixed - heat[...]
            dst[l] = mixed

    for copy in ice_rows + tracer_rows:
        copy.wait_send()

    @pl.when(has_up)
    def _():
        for copy in ice_up + [tr_up]:
            copy.wait_send()

    @pl.when(has_dn)
    def _():
        for copy in ice_dn + [tr_dn]:
            copy.wait_send()

    for copy in patches:
        copy.wait()


def write_out(*refs):
    *arrays, sems = refs
    copies = []
    for src, dst in zip(arrays[:4], arrays[4:]):
        depth = src.shape[0]
        parts = 4 if depth % 4 == 0 else 1
        for i in range(parts):
            cut = slice(i * depth // parts, (i + 1) * depth // parts)
            copies.append(
                pltpu.make_async_copy(src.at[cut], dst.at[cut], sems.at[len(copies)])
            )
            copies[-1].start()
    for copy in copies:
        copy.wait()


def per_device(
    n_grp, n_gy, pw, sa, sv, af, gvs, cc, ct, si, di, home
):
    levels, rows, cols = pw.shape
    nblock = home.shape[1]
    block_len = cols // nblock
    pair = nblock // n_gy
    ext = rows + 2 * NSUB
    f32, i32 = jnp.float32, jnp.int32
    any_space = pl.BlockSpec(memory_space=pl.ANY)
    tile = lambda *shape: pltpu.VMEM(shape, f32)
    vmem = pl.BlockSpec(memory_space=pltpu.VMEM)
    results = pl.pallas_call(
        functools.partial(kernel, n_grp, n_gy, levels, rows, cols, nblock),
        out_shape=(
            pltpu.VMEM(pw.shape, f32),
            pltpu.VMEM(sa.shape, f32),
            pltpu.VMEM(sv.shape, f32),
            pltpu.VMEM(gvs.shape, f32),
        ),
        in_specs=[pl.BlockSpec(memory_space=pltpu.SMEM)] + [any_space] * 9,
        out_specs=(vmem,) * 4,
        scratch_shapes=[
            tile(PLANES, ext, cols + LANES),
            tile(*cc.shape),
            tile(*ct.shape),
            pltpu.VMEM((rows, cols), i32),
            pltpu.VMEM((rows, cols), i32),
            tile(*pw.shape),
            tile(*sa.shape),
            tile(5, rows, cols),
            tile(rows, cols),
            pltpu.VMEM((2 * NSUB, cols), i32),
            pltpu.VMEM((8, cols), i32),
            tile(2 * levels, 8, cols),
            tile(rows, LANES),
            tile(rows, LANES),
            tile(rows, LANES),
            tile(rows, LANES),
            tile(ext, LANES),
            tile(ext, LANES),
            tile(rows, LANES),
            tile(rows, LANES),
            tile(max(n_gy - 1, 1), 5, rows, pair * block_len),
            pltpu.SemaphoreType.DMA((9,)),
            pltpu.SemaphoreType.DMA((16,)),
            pltpu.SemaphoreType.DMA((16,)),
            pltpu.SemaphoreType.DMA((8,)),
            pltpu.SemaphoreType.DMA((8,)),
            pltpu.SemaphoreType.DMA((max(n_gy - 1, 1),)),
            pltpu.SemaphoreType.DMA((max(n_gy - 1, 1),)),
        ],
        compiler_params=pltpu.CompilerParams(collective_id=0, has_side_effects=True),
    )(home, pw, sa, sv, af, gvs, cc, ct, si, di)
    return pl.pallas_call(
        write_out,
        out_shape=tuple(jax.ShapeDtypeStruct(r.shape, f32) for r in results),
        in_specs=[vmem] * 4,
        out_specs=(any_space,) * 4,
        scratch_shapes=[pltpu.SemaphoreType.DMA((10,))],
    )(*[pltpu.with_memory_space_constraint(r, pltpu.VMEM) for r in results])


def solution(mesh):
    field = P(None, "grp", "gy")
    flat = P("grp", "gy")
    return jax.shard_map(
        functools.partial(per_device, mesh.shape["grp"], mesh.shape["gy"]),
        mesh=mesh,
        in_specs=(field,) * 7 + (flat,) * 3,
        out_specs=(field,) * 4,
        check_vma=False,
    )
```

```python
import functools

import jax
import jax.numpy as jnp
from jax import lax
from jax.experimental import pallas as pl
from jax.experimental.pallas import tpu as pltpu
from jax.sharding import PartitionSpec as P

NSUB = 4
DIFFUSIVITY = 0.2
STRENGTH_COEF = 20.0
MIN_MASS = 0.5
RELAX_RATE = 0.5
ECCENTRIC = 4.0
DELTA_FLOOR = 0.0025
SPEED_FLOOR = 0.01
CORIOLIS = 0.5
HEAT_COEF = 4.0
THIN_LIMIT = 0.1
FREEZING = -1.8
WARMTH_FACTOR = 0.05
STRESS_SCALE = 0.5

LANES = 128
PLANES = 12
A_PLANE, H_PLANE, ICY_PLANE = 9, 10, 11


def shift(field, offset, axis):
    size = field.shape[axis]
    return pltpu.roll(field, (-offset) % size, axis)


def kernel(
    n_grp, n_gy, levels, rows, cols, nblock,
    home_hbm, pw, sa, sv, af, gvs, cc, ct, si, di,
    pwo, sao, cvel, glac_out,
    win, ccv, ctv, siv, div_, pwv, sav, coef, heat,
    wet_rows, halo_rows,
    pack_hi, pack_lo, tpack_hi, tpack_lo, got_hi, got_lo, tgot_hi, tgot_lo,
    picks,
    home, in_sem, row_send, row_recv, col_send, col_recv, patch_send, patch_recv,
):
    g = lax.axis_index("grp")
    y = lax.axis_index("gy")
    east = lax.rem(g + 1, n_grp)
    west = lax.rem(g + n_grp - 1, n_grp)
    has_up = y < n_gy - 1
    has_dn = y > 0
    ext = rows + 2 * NSUB
    block_len = cols // nblock
    pair = nblock // n_gy

    barrier = pltpu.get_barrier_semaphore()

    def greet(gg, yy):
        pl.semaphore_signal(
            barrier, inc=1, device_id={"grp": gg, "gy": yy},
            device_id_type=pl.DeviceIdType.MESH,
        )

    greet(east, y)
    greet(west, y)
    for k in range(1, n_gy):
        greet(g, lax.rem(y + k, n_gy))

    @pl.when(has_up)
    def _():
        greet(east, y + 1)
        greet(west, y + 1)

    @pl.when(has_dn)
    def _():
        greet(east, y - 1)
        greet(west, y - 1)

    both = jnp.where(has_up, 2, 0) + jnp.where(has_dn, 2, 0)

    center = (slice(0, rows), slice(0, cols))
    loads = [
        pltpu.make_async_copy(src, dst, in_sem.at[i])
        for i, (src, dst) in enumerate(
            (
                (cc, ccv),
                (ct, ctv),
                (di, div_),
                (si, siv),
                (gvs, win.at[0:5, 0:rows, 0:cols]),
                (sv, win.at[5:7, 0:rows, 0:cols]),
                (af, win.at[7:9, 0:rows, 0:cols]),
                (pw, pwv),
                (sa, sav),
                (home_hbm, home),
            )
        )
    ]
    for load in loads[:7]:
        load.start()

    for load in loads[:4]:
        load.wait()
    win[A_PLANE, 0:rows, 0:cols] = jnp.sum(ccv[...], axis=0)
    win[H_PLANE, 0:rows, 0:cols] = jnp.sum(ctv[...], axis=0)
    win[ICY_PLANE, 0:rows, 0:cols] = div_[...].astype(jnp.float32)
    wet = siv[...].astype(jnp.float32)
    for load in loads[4:7]:
        load.wait()
    for load in loads[7:]:
        load.start()

    pl.semaphore_wait(barrier, 1 + n_gy + both)

    def remote(src, dst, send, recv, gg, yy):
        return pltpu.make_async_remote_copy(
            src_ref=src, dst_ref=dst, send_sem=send, recv_sem=recv,
            device_id={"grp": gg, "gy": yy}, device_id_type=pl.DeviceIdType.MESH,
        )

    count = 0
    ice_rows, tracer_rows = [], []
    for to, first, at, edge, sub in (
        (west, 0, rows, 0, 7),
        (east, rows - NSUB, rows + NSUB, rows - 1, 0),
    ):
        src_rows = slice(first, first + NSUB)
        dst_rows = slice(at, at + NSUB)
        ice_pairs = ((win.at[:, src_rows, 0:cols], win.at[:, dst_rows, 0:cols]),)
        tracer_pairs = (
            (si.at[edge : edge + 1, :], wet_rows.at[sub : sub + 1, :]),
            (pw.at[:, edge : edge + 1, :], halo_rows.at[0:levels, sub : sub + 1, :]),
            (sa.at[:, edge : edge + 1, :], halo_rows.at[levels : 2 * levels, sub : sub + 1, :]),
        )
        for pairs, keep in ((ice_pairs, ice_rows), (tracer_pairs, tracer_rows)):
            for src, dst in pairs:
                keep.append(remote(src, dst, row_send.at[count], row_recv.at[count], to, y))
                count += 1
    for copy in ice_rows:
        copy.start()

    ice_up = [
        remote(pack_hi, got_lo.at[0:rows, :], col_send.at[0], col_recv.at[0], g, y + 1),
        remote(pack_hi.at[0:NSUB, :], got_lo.at[rows : rows + NSUB, :],
               col_send.at[1], col_recv.at[1], west, y + 1),
        remote(pack_hi.at[rows - NSUB : rows, :], got_lo.at[rows + NSUB : ext, :],
               col_send.at[2], col_recv.at[2], east, y + 1),
    ]
    ice_dn = [
        remote(pack_lo, got_hi.at[0:rows, :], col_send.at[3], col_recv.at[3], g, y - 1),
        remote(pack_lo.at[0:NSUB, :], got_hi.at[rows : rows + NSUB, :],
               col_send.at[4], col_recv.at[4], west, y - 1),
        remote(pack_lo.at[rows - NSUB : rows, :], got_hi.at[rows + NSUB : ext, :],
               col_send.at[5], col_recv.at[5], east, y - 1),
    ]
    tr_up = remote(tpack_hi, tgot_lo, col_send.at[6], col_recv.at[6], g, y + 1)
    tr_dn = remote(tpack_lo, tgot_hi, col_send.at[7], col_recv.at[7], g, y - 1)

    lane16 = lax.broadcasted_iota(jnp.int32, (rows, LANES), 1)

    def pack(entries):
        out = jnp.zeros((rows, LANES), jnp.float32)
        for tile, first, place, width in entries:
            moved = pltpu.roll(tile, (place - first) % LANES, 1)
            out = jnp.where((lane16 >= place) & (lane16 < place + width), moved, out)
        return out

    wet_lane = PLANES * NSUB
    hi = slice(cols - LANES, cols)
    lo = slice(0, LANES)
    pack_hi[...] = pack(
        [(win[p, 0:rows, hi], LANES - NSUB, NSUB * p, NSUB) for p in range(PLANES)]
        + [(wet[:, hi], LANES - 1, wet_lane, 1)]
    )
    pack_lo[...] = pack(
        [(win[p, 0:rows, lo], 0, NSUB * p, NSUB) for p in range(PLANES)]
        + [(wet[:, lo], 0, wet_lane, 1)]
    )

    @pl.when(has_up)
    def _():
        for copy in ice_up[1:] + ice_up[:1]:
            copy.start()

    @pl.when(has_dn)
    def _():
        for copy in ice_dn[1:] + ice_dn[:1]:
            copy.start()

    for copy in tracer_rows:
        copy.start()

    for load in loads[7:9]:
        load.wait()
    for out, cut, first in ((tpack_hi, hi, LANES - 1), (tpack_lo, lo, 0)):
        out[...] = pack(
            [(pwv[l, :, cut], first, l, 1) for l in range(levels)]
            + [(sav[l, :, cut], first, levels + l, 1) for l in range(levels)]
        )

    @pl.when(has_up)
    def _():
        tr_up.start()

    @pl.when(has_dn)
    def _():
        tr_dn.start()

    coverage = ccv[...]
    per_cat = HEAT_COEF * coverage * coverage / (ctv[...] + THIN_LIMIT * coverage)
    heat[...] = (
        (WARMTH_FACTOR * wet)
        * (win[ICY_PLANE, 0:rows, 0:cols] * (pwv[0] - FREEZING) * jnp.sum(per_cat, axis=0))
    )

    @pl.when(jnp.logical_not(has_up))
    def _():
        got_hi[...] = jnp.zeros_like(got_hi)
        tgot_hi[...] = jnp.zeros_like(tgot_hi)

    @pl.when(jnp.logical_not(has_dn))
    def _():
        got_lo[...] = jnp.zeros_like(got_lo)
        tgot_lo[...] = jnp.zeros_like(tgot_lo)

    def unpack(first, last):
        lane = lax.broadcasted_iota(jnp.int32, (last - first, LANES), 1)
        from_hi, from_lo = got_hi[first:last, :], got_lo[first:last, :]
        for p in range(PLANES):
            high = pltpu.roll(from_hi, (-NSUB * p) % LANES, 1)
            low = pltpu.roll(from_lo, (LANES - NSUB - NSUB * p) % LANES, 1)
            win[p, first:last, cols : cols + LANES] = jnp.where(
                lane < NSUB, high, jnp.where(lane >= LANES - NSUB, low, 0.0)
            )

    def columns(part):
        @pl.when(has_up)
        def _():
            for copy in ice_dn[part]:
                copy.wait_recv()

        @pl.when(has_dn)
        def _():
            for copy in ice_up[part]:
                copy.wait_recv()

    columns(slice(0, 1))
    unpack(0, rows)
    columns(slice(1, 3))
    unpack(rows, ext)
    for copy in ice_rows:
        copy.wait_recv()

    vel_u, vel_v = win[0], win[1]
    sig_one, sig_two, sig_shear = win[2], win[3], win[4]
    cur_u, cur_v, wind_u, wind_v = win[5], win[6], win[7], win[8]
    conc, thick, icy = win[A_PLANE], win[H_PLANE], win[ICY_PLANE]
    strength = thick * jnp.exp(-STRENGTH_COEF * (1.0 - conc))
    mass = thick + MIN_MASS
    keep = icy * (1.0 / (1.0 + RELAX_RATE))
    push = keep * strength * RELAX_RATE
    push_dev = push * (1.0 / ECCENTRIC)

    def drag(u, v):
        square = (cur_u - u) ** 2 + (cur_v - v) ** 2 + SPEED_FLOOR
        return conc * (square * lax.rsqrt(square))

    for _ in range(NSUB):
        u_east = shift(vel_u, 1, 0) - vel_u
        v_north = shift(vel_v, 1, 1) - vel_v
        u_north = shift(vel_u, 1, 1) - vel_u
        v_east = shift(vel_v, 1, 0) - vel_v
        diverge = u_east + v_north
        tension = u_east - v_north
        shear = u_north + v_east
        inverse = lax.rsqrt(
            diverge * diverge
            + (tension * tension + shear * shear) * (1.0 / ECCENTRIC)
            + DELTA_FLOOR
        )
        sig_one = keep * sig_one + push * (diverge * inverse - 1.0)
        scaled = push_dev * inverse
        sig_two = keep * sig_two + scaled * tension
        sig_shear = keep * sig_shear + scaled * shear
        total = sig_one + sig_two
        differ = sig_one - sig_two
        force_u = 0.5 * (total - shift(total, -1, 0)) + (sig_shear - shift(sig_shear, -1, 1))
        force_v = 0.5 * (differ - shift(differ, -1, 1)) + (sig_shear - shift(sig_shear, -1, 0))
        water = drag(vel_u, vel_v)
        scale = icy / (mass + water)
        turn_u = (CORIOLIS * mass) * vel_v
        turn_v = (CORIOLIS * mass) * vel_u
        new_u = (mass * vel_u + force_u + wind_u + water * cur_u + turn_u) * scale
        new_v = (mass * vel_v + force_v + wind_v + water * cur_v - turn_v) * scale
        vel_u, vel_v = new_u, new_v

    state = [f[0:rows, 0:cols] for f in (vel_u, vel_v, sig_one, sig_two, sig_shear)]

    loads[9].wait()
    homes = [home[0, b] for b in range(nblock)]

    def choose(slot, field):
        out = jnp.zeros((rows, block_len), jnp.float32)
        for b in range(nblock):
            out = jnp.where(homes[b] == slot, field[:, b * block_len : (b + 1) * block_len], out)
        return out

    span = pair * block_len
    place = pl.ds(pl.multiple_of(y * span, LANES), span)
    patches = []
    for k in range(1, n_gy):
        peer = lax.rem(y + k, n_gy)
        for f in range(5):
            for p in range(pair):
                picks[k - 1, f, :, p * block_len : (p + 1) * block_len] = choose(
                    peer * pair + p, state[f]
                )
        copy = remote(
            picks.at[k - 1], glac_out.at[:, :, place],
            patch_send.at[k - 1], patch_recv.at[k - 1], g, peer,
        )
        copy.start()
        patches.append(copy)
    for f in range(5):
        for p in range(pair):
            glac_out[f, :, pl.ds(pl.multiple_of(y * span + p * block_len, LANES), block_len)] = (
                choose(y * pair + p, state[f])
            )

    wide_u = icy * drag(vel_u, vel_v)
    tau_u = (wide_u * (vel_u - cur_u))[0:rows, 0:cols]
    tau_v = (wide_u * (vel_v - cur_v))[0:rows, 0:cols]
    cvel[0] = wet * (cur_u[0:rows, 0:cols] + STRESS_SCALE * tau_u)
    cvel[1] = wet * (cur_v[0:rows, 0:cols] + STRESS_SCALE * tau_v)

    for copy in tracer_rows:
        copy.wait_recv()

    @pl.when(has_up)
    def _():
        tr_dn.wait_recv()

    @pl.when(has_dn)
    def _():
        tr_up.wait_recv()

    row = lax.broadcasted_iota(jnp.int32, (rows, cols), 0)
    lane = lax.broadcasted_iota(jnp.int32, (rows, cols), 1)
    reps = cols // LANES

    def neighbours(field, edge_rows, high, low):
        edge = jnp.concatenate([edge_rows] * (rows // 8), axis=0)
        high = jnp.concatenate([high] * reps, axis=1)
        low = jnp.concatenate([low] * reps, axis=1)
        return (
            jnp.where(row == rows - 1, edge, shift(field, 1, 0)),
            jnp.where(row == 0, edge, shift(field, -1, 0)),
            jnp.where(lane == cols - 1, high, shift(field, 1, 1)),
            jnp.where(lane == 0, low, shift(field, -1, 1)),
        )

    near = neighbours(
        wet,
        wet_rows[...].astype(jnp.float32),
        pltpu.roll(got_hi[0:rows, :], (LANES - 1 - wet_lane) % LANES, 1),
        pltpu.roll(got_lo[0:rows, :], (-wet_lane) % LANES, 1),
    )
    rate = DIFFUSIVITY * wet
    weights = [rate * n for n in near]
    for i in range(4):
        coef[i] = weights[i]
    coef[4] = 1.0 - (weights[0] + weights[1] + weights[2] + weights[3])

    thi, tlo = tgot_hi[...], tgot_lo[...]
    for src, dst, base in ((pwv, pwo, 0), (sav, sao, levels)):
        for l in range(levels):
            at = base + l
            field = src[l]
            sides = neighbours(
                field,
                halo_rows[at],
                pltpu.roll(thi, (LANES - 1 - at) % LANES, 1),
                pltpu.roll(tlo, (-at) % LANES, 1),
            )
            mixed = coef[4] * field
            for i in range(4):
                mixed = mixed + coef[i] * sides[i]
            if at == 0:
                mixed = mixed - heat[...]
            dst[l] = mixed

    for copy in ice_rows + tracer_rows:
        copy.wait_send()

    @pl.when(has_up)
    def _():
        for copy in ice_up + [tr_up]:
            copy.wait_send()

    @pl.when(has_dn)
    def _():
        for copy in ice_dn + [tr_dn]:
            copy.wait_send()

    for copy in patches:
        copy.wait()


def write_out(*refs):
    *arrays, sems = refs
    copies = []
    for src, dst in zip(arrays[:4], arrays[4:]):
        depth = src.shape[0]
        parts = 4 if depth % 4 == 0 else 1
        for i in range(parts):
            cut = slice(i * depth // parts, (i + 1) * depth // parts)
            copies.append(
                pltpu.make_async_copy(src.at[cut], dst.at[cut], sems.at[len(copies)])
            )
            copies[-1].start()
    for copy in copies:
        copy.wait()


def per_device(
    n_grp, n_gy, pw, sa, sv, af, gvs, cc, ct, si, di, home
):
    levels, rows, cols = pw.shape
    nblock = home.shape[1]
    block_len = cols // nblock
    pair = nblock // n_gy
    ext = rows + 2 * NSUB
    f32, i32 = jnp.float32, jnp.int32
    any_space = pl.BlockSpec(memory_space=pl.ANY)
    tile = lambda *shape: pltpu.VMEM(shape, f32)
    vmem = pl.BlockSpec(memory_space=pltpu.VMEM)
    results = pl.pallas_call(
        functools.partial(kernel, n_grp, n_gy, levels, rows, cols, nblock),
        out_shape=(
            pltpu.VMEM(pw.shape, f32),
            pltpu.VMEM(sa.shape, f32),
            pltpu.VMEM(sv.shape, f32),
            pltpu.VMEM(gvs.shape, f32),
        ),
        in_specs=[any_space] * 10,
        out_specs=(vmem,) * 4,
        scratch_shapes=[
            tile(PLANES, ext, cols + LANES),
            tile(*cc.shape),
            tile(*ct.shape),
            pltpu.VMEM((rows, cols), i32),
            pltpu.VMEM((rows, cols), i32),
            tile(*pw.shape),
            tile(*sa.shape),
            tile(5, rows, cols),
            tile(rows, cols),
            pltpu.VMEM((8, cols), i32),
            tile(2 * levels, 8, cols),
            tile(rows, LANES),
            tile(rows, LANES),
            tile(rows, LANES),
            tile(rows, LANES),
            tile(ext, LANES),
            tile(ext, LANES),
            tile(rows, LANES),
            tile(rows, LANES),
            tile(max(n_gy - 1, 1), 5, rows, pair * block_len),
            pltpu.SMEM(home.shape, i32),
            pltpu.SemaphoreType.DMA((10,)),
            pltpu.SemaphoreType.DMA((8,)),
            pltpu.SemaphoreType.DMA((8,)),
            pltpu.SemaphoreType.DMA((8,)),
            pltpu.SemaphoreType.DMA((8,)),
            pltpu.SemaphoreType.DMA((max(n_gy - 1, 1),)),
            pltpu.SemaphoreType.DMA((max(n_gy - 1, 1),)),
        ],
        compiler_params=pltpu.CompilerParams(collective_id=0, has_side_effects=True),
    )(home, pw, sa, sv, af, gvs, cc, ct, si, di)
    return pl.pallas_call(
        write_out,
        out_shape=tuple(jax.ShapeDtypeStruct(r.shape, f32) for r in results),
        in_specs=[vmem] * 4,
        out_specs=(any_space,) * 4,
        scratch_shapes=[pltpu.SemaphoreType.DMA((10,))],
    )(*[pltpu.with_memory_space_constraint(r, pltpu.VMEM) for r in results])


def solution(mesh):
    field = P(None, "grp", "gy")
    flat = P("grp", "gy")
    return jax.shard_map(
        functools.partial(per_device, mesh.shape["grp"], mesh.shape["gy"]),
        mesh=mesh,
        in_specs=(field,) * 7 + (flat,) * 3,
        out_specs=(field,) * 4,
        check_vma=False,
    )
```
